512 devices in a mesh: snap: 32 (over z, x), vert: 16 (over y, core).
Axes of the slice: x: 4, y: 8, z: 8, core: 2. Of those that a mesh axis runs over, the one named last changes fastest.
Arguments:
- features: bfloat16 [32, 4096, 512], P('snap', 'vert'), may hold values from -6 to 6
- tile_values: bfloat16 [32, 32, 12, 128, 128], P('snap', 'vert'), may hold values from -0.21875 to 0.21875
- tile_column: int32 [32, 32, 12], P('snap', 'vert'), may hold values from 0 to 31
- tile_count: int32 [32, 32], P('snap', 'vert'), may hold values from 1 to 12, 192 in all within a row
- message_one: bfloat16 [512, 512], replicated, may hold values from -0.25 to 0.25
- root_one: bfloat16 [512, 512], replicated, may hold values from -0.25 to 0.25
- time_taps: float32 [16, 512], replicated, may hold values from -1.5 to 1.5
- message_two: bfloat16 [512, 512], replicated, may hold values from -0.25 to 0.25
- root_two: bfloat16 [512, 512], replicated, may hold values from -0.25 to 0.25
Outputs:
- embedding: bfloat16 [32, 4096, 512], P('snap', 'vert')
The draws below stay inside these ranges and needn't reach their ends.
Inputs may be any that keep to these rules, and one draw needn't show every extreme that they name: `tile_count`: over one snapshot the counts sum to 192, and some row block has 12 live slots; slots at or past the count are ignored. `tile_column`: blocks may repeat within a row block's list.
All inputs are finite; a program needn't handle non-finite values.
Results may differ from the reference program's by a relative error of at most 0.0064.
Values may be sent and summed in bfloat16 or wider, within the bound.
No kernel may reach another device: no remote copies, remote signals or barrier semaphores. Data moves between devices by JAX's collectives and lax.ppermute only.
A program may use at most 64 MiB of HBM per device.

```python
import math
import jax
import jax.numpy as jnp
import numpy as np
from jax import lax

WIDTH = 512
TILE = 128
SLOTS = 12
TAPS = 16
SNAPS = 32
BLOCKS = 32
VERTS = 4096


def touch_ends(entries, rng, least, high):
    shape = entries.shape
    spot = [jax.random.randint(jax.random.fold_in(rng, axis), (), 0, shape[axis]) for axis in range(len(shape))]
    entries = entries.at[tuple(spot)].set(least)
    longest = shape.index(max(shape))
    spot[longest] = (spot[longest] + 1) % shape[longest]
    return entries.at[tuple(spot)].set(high)


def levels(rng, dims, split, smallest, top_value):
    def one(position, shards_of):
        draws = jax.random.uniform(jax.random.fold_in(jax.random.fold_in(rng, 6), position), (shards_of,), jnp.float32, smallest / len(split), top_value / len(split))
        return jnp.repeat(jnp.exp(draws), dims[position] // shards_of).reshape((-1,) + (1,) * (len(dims) - position - 1))

    level = one(*split[0])
    for cut in split[1:]:
        level = level * one(*cut)
    return level


def profile(amount, total, reach, skew):
    portions = [(1 << 20) // math.isqrt(standing ** skew) + 1 for standing in range(2, amount + 1)]
    rest, holding = total - reach - (amount - 1), [1] * (amount - 1)
    while rest > 0:
        free = [i for i in range(amount - 1) if holding[i] < reach]
        whole, budget = sum([portions[i] for i in free]), rest
        for i in free:
            extra = min(reach - holding[i], max(1, budget * portions[i] // whole), rest)
            holding[i] = holding[i] + extra
            rest = rest - extra
    return np.array([reach] + holding)


def uneven(stream_key, number_of, total, reach, lean):
    if number_of == 2:
        one = jax.random.randint(stream_key, (), max(1, total - reach), min(reach, total - 1) + 1)
        return jnp.stack([one, total - one])
    sizes = jnp.asarray(profile(number_of, total, reach, lean), jnp.int32)
    pairs = (number_of - 1) // 2
    donor, sink = sizes[1:1 + 2 * pairs:2], sizes[2:2 + 2 * pairs:2]
    slack = jnp.minimum(donor - 1, reach - sink)
    moved = jax.random.randint(jax.random.fold_in(stream_key, 1), (pairs,), 0, 1 << 20) % (slack + 1)
    sizes = sizes.at[1:1 + 2 * pairs:2].set(donor - moved).at[2:2 + 2 * pairs:2].set(sink + moved)
    return sizes[jax.random.permutation(jax.random.fold_in(stream_key, 2), number_of)]


def gaussian(rng, dims, width, most, shards=(), kind=jnp.bfloat16):
    values = jax.random.normal(rng, dims, jnp.float32) * width
    if len(shards) > 0:
        values = levels(rng, dims, shards, -0.22, 0.18) * values
    return jnp.clip(values, min=-most, max=most).astype(kind)


def setup_inputs(seed: int = 0) -> dict:
    arg_keys = jax.random.split(jax.random.key(seed), 10)
    return {
        "features": gaussian(arg_keys[0], (SNAPS, VERTS, WIDTH), 1.0, 6.0, ((0, 32), (1, 16))),
        "tile_values": gaussian(arg_keys[1], (SNAPS, BLOCKS, SLOTS, TILE, TILE), (TILE * SLOTS // 2) ** -0.5, 0.21875, ((0, 32), (1, 16))),
        "tile_column": touch_ends(jax.random.randint(arg_keys[2], (SNAPS, BLOCKS, SLOTS), 0, BLOCKS), jax.random.fold_in(arg_keys[2], 1), 0, BLOCKS - 1).astype(jnp.int32),
        "tile_count": jax.vmap(lambda own: uneven(own, BLOCKS, BLOCKS * SLOTS // 2, SLOTS, 2))(jax.random.split(arg_keys[3], SNAPS)).reshape((SNAPS, BLOCKS)).astype(jnp.int32),
        "message_one": gaussian(arg_keys[4], (WIDTH, WIDTH), WIDTH ** -0.5, 0.25),
        "root_one": gaussian(arg_keys[5], (WIDTH, WIDTH), WIDTH ** -0.5, 0.25),
        "time_taps": gaussian(arg_keys[6], (TAPS, WIDTH), 0.25, 1.5, (), jnp.float32),
        "message_two": gaussian(arg_keys[7], (WIDTH, WIDTH), WIDTH ** -0.5, 0.25),
        "root_two": gaussian(arg_keys[8], (WIDTH, WIDTH), WIDTH ** -0.5, 0.25),
    }


def graph_layer(inputs, tiles, columns, counts, w_message, w_root):
    messages = jnp.dot(inputs, w_message, preferred_element_type=jnp.float32).astype(jnp.bfloat16)
    blocks = messages.astype(jnp.float32).reshape(BLOCKS, TILE, WIDTH)
    live = (jnp.arange(SLOTS, dtype=jnp.int32)[None, :] < counts[:, None]).astype(jnp.float32)
    picked = blocks[columns.astype(jnp.int32)] * live[:, :, None, None]
    summed = jnp.einsum('rkij,rkjf->rif', tiles.astype(jnp.float32), picked).reshape(VERTS, WIDTH)
    total = summed + jnp.dot(inputs, w_root, preferred_element_type=jnp.float32)
    return jnp.maximum(total, 0.0).astype(jnp.bfloat16)


def reference(features, tile_values, tile_column, tile_count, message_one, root_one, time_taps, message_two, root_two):
    hidden = lax.map(lambda item: graph_layer(item[0], item[1], item[2], item[3], message_one, root_one),
                     (features, tile_values, tile_column, tile_count))
    wide = hidden.astype(jnp.float32)
    padded = jnp.concatenate([jnp.zeros((TAPS - 1, VERTS, WIDTH), jnp.float32), wide], 0)
    mixed = jnp.zeros((SNAPS, VERTS, WIDTH), jnp.float32)
    for offset in range(TAPS):
        mixed = mixed + time_taps[offset][None, None, :] * padded[TAPS - 1 - offset:TAPS - 1 - offset + SNAPS]
    mixed = mixed.astype(jnp.bfloat16)
    return lax.map(lambda item: graph_layer(item[0], item[1], item[2], item[3], message_two, root_two),
                   (mixed, tile_values, tile_column, tile_count))
```

```python
import jax
import jax.numpy as jnp
from jax import lax
from jax.experimental import pallas as pl
from jax.experimental.pallas import tpu as pltpu
from jax.sharding import PartitionSpec as P

TILE = 128
TAPS = 16


def layer_kernel(cols, counts, tiles, gathered, own, w_message, w_root, out, total):
    for r in range(2):
        total[r] = jnp.zeros(total.shape[1:], jnp.float32)

        @pl.loop(0, counts[r])
        def _(k):
            total[r] += jnp.dot(
                tiles[r, k], gathered[cols[r, k]], preferred_element_type=jnp.float32
            )

        rows = pl.ds(r * TILE, TILE)
        full = jnp.dot(
            total[r].astype(jnp.bfloat16), w_message[...], preferred_element_type=jnp.float32
        ) + jnp.dot(own[rows, :], w_root[...], preferred_element_type=jnp.float32)
        out[rows, :] = jnp.maximum(full, 0.0).astype(jnp.bfloat16)


def graph_layer(inputs, tiles, columns, counts, w_message, w_root):
    rows, width = inputs.shape
    gathered = lax.all_gather(inputs, "vert", axis=0, tiled=True)
    gathered = gathered.reshape(-1, TILE, width)
    smem = pl.BlockSpec(memory_space=pltpu.SMEM)
    vmem = pl.BlockSpec(memory_space=pltpu.VMEM)
    return pl.pallas_call(
        layer_kernel,
        out_shape=jax.ShapeDtypeStruct((rows, width), jnp.bfloat16),
        in_specs=[smem, smem, vmem, vmem, vmem, vmem, vmem],
        out_specs=vmem,
        scratch_shapes=[pltpu.VMEM((2, TILE, width), jnp.float32)],
        compiler_params=pltpu.CompilerParams(vmem_limit_bytes=24 << 20),
        name="layer",
    )(columns, counts, tiles, gathered, inputs, w_message, w_root)


def filter_kernel(hidden, taps, out):
    steps = hidden.shape[0]
    for t in range(steps):
        acc = taps[0:1, :] * hidden[t].astype(jnp.float32)
        for j in range(1, min(TAPS - 1, t) + 1):
            acc = acc + taps[j : j + 1, :] * hidden[t - j].astype(jnp.float32)
        out[t] = acc.astype(jnp.bfloat16)


def temporal(hidden, taps):
    rows, width = hidden.shape
    steps = lax.axis_size("snap")
    split = hidden.reshape(steps, rows // steps, width)
    by_vertex = lax.all_to_all(split, "snap", split_axis=0, concat_axis=0)
    vmem = pl.BlockSpec(memory_space=pltpu.VMEM)
    mixed = pl.pallas_call(
        filter_kernel,
        out_shape=jax.ShapeDtypeStruct(by_vertex.shape, jnp.bfloat16),
        in_specs=[vmem, vmem],
        out_specs=vmem,
        name="temporal",
    )(by_vertex, taps)
    returned = lax.all_to_all(mixed, "snap", split_axis=0, concat_axis=0)
    return returned.reshape(rows, width)


def shards(
    features,
    tile_values,
    tile_column,
    tile_count,
    message_one,
    root_one,
    time_taps,
    message_two,
    root_two,
):
    tiles, columns, counts = tile_values[0], tile_column[0], tile_count[0]
    hidden = graph_layer(features[0], tiles, columns, counts, message_one, root_one)
    mixed = temporal(hidden, time_taps)
    out = graph_layer(mixed, tiles, columns, counts, message_two, root_two)
    return out[None]


def solution(mesh):
    return jax.shard_map(
        shards,
        mesh=mesh,
        in_specs=(
            P("snap", "vert", None),
            P("snap", "vert", None, None, None),
            P("snap", "vert", None),
            P("snap", "vert"),
            P(),
            P(),
            P(),
            P(),
            P(),
        ),
        out_specs=P("snap", "vert", None),
        check_vma=False,
    )
```

```python
import functools

import jax
import jax.numpy as jnp
from jax import lax
from jax.experimental import pallas as pl
from jax.experimental.pallas import tpu as pltpu
from jax.sharding import PartitionSpec as P

TILE = 128
TAPS = 16
RING = 8
SMEM = pl.BlockSpec(memory_space=pltpu.SMEM)
VMEM = pl.BlockSpec(memory_space=pltpu.VMEM)


def call(kernel, outs, operands, specs, name, flops, moved, aliases={}, scratch=()):
    return pl.pallas_call(
        kernel,
        out_shape=outs,
        in_specs=specs,
        out_specs=jax.tree.map(lambda _: VMEM, outs),
        scratch_shapes=scratch,
        input_output_aliases=aliases,
        cost_estimate=pl.CostEstimate(flops=flops, bytes_accessed=moved, transcendentals=0),
        compiler_params=pltpu.CompilerParams(vmem_limit_bytes=16 << 20),
        name=name,
    )(*operands)


def plan_kernel(slots, where, own, partner, plan):
    y, core = where[0] // 2, where[0] % 2
    lists = 2 * RING
    for i in range(lists):
        plan[i] = 0
    for side, table in enumerate((own, partner)):
        for r in range(2):

            @pl.loop(0, table[r * (slots + 1) + slots])
            def _(k):
                column = table[r * (slots + 1) + k]
                near = lax.rem(column // 4 - y + RING, RING) * 2 + side

                @pl.when(lax.rem(column // 2, 2) == core)
                def _():
                    filled = plan[near]
                    plan[lists + near * 2 * slots + filled] = (r * slots + k) * 2 + lax.rem(
                        column, 2
                    )
                    plan[near] = filled + 1


def add_tiles(plan, pieces, tiles, sums):
    slots = tiles[0].shape[0] // 2
    for near, piece in pieces:
        for side in range(2):
            index = near * 2 + side

            @pl.loop(0, plan[index])
            def _(i):
                entry = plan[2 * RING + index * 2 * slots + i]
                half, slot = lax.rem(entry, 2), entry // 2
                rows = pl.ds(pl.multiple_of(slot // slots * TILE, TILE), TILE)
                block = pl.ds(pl.multiple_of(half * TILE, TILE), TILE)
                sums[side][rows, :] += jnp.dot(
                    tiles[side][slot], piece[block, :], preferred_element_type=jnp.float32
                )


def early_kernel(plan, p0, p1, p2, p6, p7, own_tiles, other_tiles, w_root, mine, theirs, root):
    mine[...] = jnp.zeros_like(mine)
    theirs[...] = jnp.zeros_like(theirs)
    pieces = ((0, p0), (1, p1), (7, p7), (2, p2), (6, p6))
    add_tiles(plan, pieces, (own_tiles, other_tiles), (mine, theirs))
    root[...] = jnp.dot(p0[...], w_root[...], preferred_element_type=jnp.float32)


def late_kernel(plan, p3, p4, p5, own_tiles, other_tiles, mine_in, theirs_in, mine, theirs):
    mine[...] = mine_in[...]
    theirs[...] = theirs_in[...]
    add_tiles(plan, ((3, p3), (4, p4), (5, p5)), (own_tiles, other_tiles), (mine, theirs))


def last_kernel(mine, received, root, w_message, out):
    total = (mine[...] + received[...]).astype(jnp.bfloat16)
    full = jnp.dot(total, w_message[...], preferred_element_type=jnp.float32) + root[...]
    out[...] = jnp.maximum(full, 0.0).astype(jnp.bfloat16)


def moves(up, down):
    return [(2 * y, (2 * y + 2 * up) % (2 * RING)) for y in range(RING)] + [
        (2 * y + 1, (2 * y + 2 * down) % (2 * RING) + 1) for y in range(RING)
    ]


def shift(x, distance):
    return lax.ppermute(x, "vert", moves(distance, distance))


def swap(x):
    return lax.ppermute(x, "vert", [(v, v ^ 1) for v in range(2 * RING)])


def ring_gather(own):
    first = lax.rem(lax.axis_index("vert"), 2) == 0
    up2, down2 = shift(own, 2), shift(own, -2)
    up1, down1 = shift(own, 1), shift(own, -1)
    up3, down3 = shift(up2, 1), shift(down2, -1)
    across = lax.ppermute(jnp.where(first, up2, down2), "vert", moves(2, -2))
    return (own, down1, down2, down3, across, up3, up2, up1)


def graph_layer(pieces, own_tiles, other_tiles, plan, w_message, w_root):
    own = pieces[0]
    rows, width = own.shape
    sums = jax.ShapeDtypeStruct((rows, width), jnp.float32)
    area = rows * width
    dense = 2 * area * width
    mine, theirs, root = call(
        early_kernel,
        (sums, sums, sums),
        (plan, own, pieces[1], pieces[2], pieces[6], pieces[7], own_tiles, other_tiles, w_root),
        [SMEM] + [VMEM] * 8,
        "early",
        4 * dense,
        24 * area,
    )
    mine, theirs = call(
        late_kernel,
        (sums, sums),
        (plan, pieces[3], pieces[4], pieces[5], own_tiles, other_tiles, mine, theirs),
        [SMEM] + [VMEM] * 7,
        "late",
        2 * dense,
        16 * area,
        aliases={6: 0, 7: 1},
    )
    received = swap(theirs)
    return call(
        last_kernel,
        jax.ShapeDtypeStruct((rows, width), jnp.bfloat16),
        (mine, received, root, w_message),
        [VMEM] * 4,
        "last",
        dense,
        14 * area,
    )


def filter_kernel(hidden, taps, out):
    steps = hidden.shape[0]
    for t in range(steps):
        acc = taps[0:1, :] * hidden[t].astype(jnp.float32)
        for j in range(1, min(TAPS - 1, t) + 1):
            acc = acc + taps[j : j + 1, :] * hidden[t - j].astype(jnp.float32)
        out[t] = acc.astype(jnp.bfloat16)


def temporal(hidden, taps):
    rows, width = hidden.shape
    steps = lax.axis_size("snap")
    split = hidden.reshape(steps, rows // steps, width)
    by_vertex = lax.all_to_all(split, "snap", split_axis=0, concat_axis=0)
    mixed = call(
        filter_kernel,
        jax.ShapeDtypeStruct(by_vertex.shape, jnp.bfloat16),
        (by_vertex, taps),
        [VMEM] * 2,
        "temporal",
        32 * rows * width,
        4 * rows * width,
    )
    returned = lax.all_to_all(mixed, "snap", split_axis=0, concat_axis=0)
    return returned.reshape(rows, width)


def shards(
    features,
    tile_values,
    tile_column,
    tile_count,
    message_one,
    root_one,
    time_taps,
    message_two,
    root_two,
):
    slots = tile_column.shape[2]
    own_tiles = tile_values[0].reshape(2 * slots, TILE, TILE)
    table = jnp.concatenate([tile_column[0], tile_count[0][:, None]], 1).reshape(-1)
    pieces = ring_gather(features[0])
    tiles_out, table_out, _ = lax.optimization_barrier((own_tiles, table, pieces[1]))
    other_tiles, other_table = swap(tiles_out), swap(table_out)
    plan = pl.pallas_call(
        functools.partial(plan_kernel, slots),
        out_shape=jax.ShapeDtypeStruct((2 * RING * (2 * slots + 1),), jnp.int32),
        in_specs=[SMEM] * 3,
        out_specs=SMEM,
        cost_estimate=pl.CostEstimate(flops=1000, bytes_accessed=4000, transcendentals=0),
        name="plan",
    )(lax.axis_index("vert").reshape(1), table, other_table)
    hidden = graph_layer(pieces, own_tiles, other_tiles, plan, message_one, root_one)
    mixed = temporal(hidden, time_taps)
    pieces = ring_gather(mixed)
    out = graph_layer(pieces, own_tiles, other_tiles, plan, message_two, root_two)
    return out[None]


def solution(mesh):
    return jax.shard_map(
        shards,
        mesh=mesh,
        in_specs=(
            P("snap", "vert", None),
            P("snap", "vert", None, None, None),
            P("snap", "vert", None),
            P("snap", "vert"),
            P(),
            P(),
            P(),
            P(),
            P(),
        ),
        out_specs=P("snap", "vert", None),
        check_vma=False,
    )
```

```python
import functools

import jax
import jax.numpy as jnp
from jax import lax
from jax.experimental import pallas as pl
from jax.experimental.pallas import tpu as pltpu
from jax.sharding import PartitionSpec as P

TILE = 128
TAPS = 16
RING = 8
SMEM = pl.BlockSpec(memory_space=pltpu.SMEM)
VMEM = pl.BlockSpec(memory_space=pltpu.VMEM)


def call(kernel, outs, operands, specs, flops, moved, aliases={}, scratch=()):
    return pl.pallas_call(
        kernel,
        out_shape=outs,
        in_specs=specs,
        out_specs=jax.tree.map(lambda _: VMEM, outs),
        scratch_shapes=scratch,
        input_output_aliases=aliases,
        cost_estimate=pl.CostEstimate(flops=flops, bytes_accessed=moved, transcendentals=0),
        compiler_params=pltpu.CompilerParams(vmem_limit_bytes=16 << 20),
    )(*operands)


def plan_kernel(slots, where, own, partner, plan):
    y, core = where[0] // 2, where[0] % 2
    lists = 2 * RING
    for i in range(lists):
        plan[i] = 0
    for side, table in enumerate((own, partner)):
        for r in range(2):

            @pl.loop(0, table[r * (slots + 1) + slots])
            def _(k):
                column = table[r * (slots + 1) + k]
                near = lax.rem(column // 4 - y + RING, RING) * 2 + side

                @pl.when(lax.rem(column // 2, 2) == core)
                def _():
                    filled = plan[near]
                    plan[lists + near * 2 * slots + filled] = (r * slots + k) * 2 + lax.rem(
                        column, 2
                    )
                    plan[near] = filled + 1


def add_tiles(plan, pieces, tiles, sums):
    for near, piece in pieces:
        for side in tiles:
            slots = tiles[side].shape[0] // 2
            index = near * 2 + side

            @pl.loop(0, plan[index])
            def _(i):
                entry = plan[2 * RING + index * 2 * slots + i]
                half, slot = lax.rem(entry, 2), entry // 2
                rows = pl.ds(pl.multiple_of(slot // slots * TILE, TILE), TILE)
                block = pl.ds(pl.multiple_of(half * TILE, TILE), TILE)
                sums[side][rows, :] += jnp.dot(
                    tiles[side][slot], piece[block, :], preferred_element_type=jnp.float32
                )


def early_kernel(plan, p0, p1, p2, p6, p7, own_tiles, other_tiles, w_root, mine, theirs, root):
    mine[...] = jnp.zeros_like(mine)
    theirs[...] = jnp.zeros_like(theirs)
    pieces = ((0, p0), (1, p1), (7, p7), (2, p2), (6, p6))
    add_tiles(plan, pieces, {0: own_tiles, 1: other_tiles}, {0: mine, 1: theirs})
    root[...] = jnp.dot(p0[...], w_root[...], preferred_element_type=jnp.float32)


def late_kernel(plan, p3, p4, p5, tiles, sums_in, sums, *, side):
    sums[...] = sums_in[...]
    add_tiles(plan, ((3, p3), (4, p4), (5, p5)), {side: tiles}, {side: sums})


def last_kernel(mine, received, root, w_message, out):
    total = (mine[...] + received[...]).astype(jnp.bfloat16)
    full = jnp.dot(total, w_message[...], preferred_element_type=jnp.float32) + root[...]
    out[...] = jnp.maximum(full, 0.0).astype(jnp.bfloat16)


def moves(up, down):
    return [(2 * y, (2 * y + 2 * up) % (2 * RING)) for y in range(RING)] + [
        (2 * y + 1, (2 * y + 2 * down) % (2 * RING) + 1) for y in range(RING)
    ]


def shift(x, distance):
    return lax.ppermute(x, "vert", moves(distance, distance))


def swap(x):
    return lax.ppermute(x, "vert", [(v, v ^ 1) for v in range(2 * RING)])


def ring_gather(own):
    first = lax.rem(lax.axis_index("vert"), 2) == 0
    up2, down2 = shift(own, 2), shift(own, -2)
    up1, down1 = shift(own, 1), shift(own, -1)
    up3, down3 = shift(up2, 1), shift(down2, -1)
    across = lax.ppermute(jnp.where(first, up2, down2), "vert", moves(2, -2))
    return (own, down1, down2, down3, across, up3, up2, up1)


def graph_layer(pieces, own_tiles, other_tiles, plan, w_message, w_root):
    own = pieces[0]
    rows, width = own.shape
    sums = jax.ShapeDtypeStruct((rows, width), jnp.float32)
    area = rows * width
    dense = 2 * area * width
    mine, theirs, root = call(
        early_kernel,
        (sums, sums, sums),
        (plan, own, pieces[1], pieces[2], pieces[6], pieces[7], own_tiles, other_tiles, w_root),
        [SMEM] + [VMEM] * 8,
        4 * dense,
        24 * area,
    )
    late = pieces[3:6]

    def finish(side, tiles, partial):
        return call(
            functools.partial(late_kernel, side=side),
            sums,
            (plan, *late, tiles, partial),
            [SMEM] + [VMEM] * 5,
            dense,
            8 * area,
            aliases={5: 0},
        )

    received = swap(finish(1, other_tiles, theirs))
    mine = finish(0, own_tiles, mine)
    return call(
        last_kernel,
        jax.ShapeDtypeStruct((rows, width), jnp.bfloat16),
        (mine, received, root, w_message),
        [VMEM] * 4,
        dense,
        14 * area,
    )


def filter_kernel(hidden, taps, out):
    steps = hidden.shape[0]
    for t in range(steps):
        acc = taps[0:1, :] * hidden[t].astype(jnp.float32)
        for j in range(1, min(TAPS - 1, t) + 1):
            acc = acc + taps[j : j + 1, :] * hidden[t - j].astype(jnp.float32)
        out[t] = acc.astype(jnp.bfloat16)


def temporal(hidden, taps):
    rows, width = hidden.shape
    steps = lax.axis_size("snap")
    split = hidden.reshape(steps, rows // steps, width)
    by_vertex = lax.all_to_all(split, "snap", split_axis=0, concat_axis=0)
    mixed = call(
        filter_kernel,
        jax.ShapeDtypeStruct(by_vertex.shape, jnp.bfloat16),
        (by_vertex, taps),
        [VMEM] * 2,
        32 * rows * width,
        4 * rows * width,
    )
    returned = lax.all_to_all(mixed, "snap", split_axis=0, concat_axis=0)
    return returned.reshape(rows, width)


def shards(
    features,
    tile_values,
    tile_column,
    tile_count,
    message_one,
    root_one,
    time_taps,
    message_two,
    root_two,
):
    slots = tile_column.shape[2]
    own_tiles = tile_values[0].reshape(2 * slots, TILE, TILE)
    table = jnp.concatenate([tile_column[0], tile_count[0][:, None]], 1).reshape(-1)
    pieces = ring_gather(features[0])
    other_tiles, other_table = swap(own_tiles), swap(table)
    plan = pl.pallas_call(
        functools.partial(plan_kernel, slots),
        out_shape=jax.ShapeDtypeStruct((2 * RING * (2 * slots + 1),), jnp.int32),
        in_specs=[SMEM] * 3,
        out_specs=SMEM,
        cost_estimate=pl.CostEstimate(flops=1000, bytes_accessed=4000, transcendentals=0),
        name="plan",
    )(lax.axis_index("vert").reshape(1), table, other_table)
    hidden = graph_layer(pieces, own_tiles, other_tiles, plan, message_one, root_one)
    mixed = temporal(hidden, time_taps)
    pieces = ring_gather(mixed)
    out = graph_layer(pieces, own_tiles, other_tiles, plan, message_two, root_two)
    return out[None]


def solution(mesh):
    return jax.shard_map(
        shards,
        mesh=mesh,
        in_specs=(
            P("snap", "vert", None),
            P("snap", "vert", None, None, None),
            P("snap", "vert", None),
            P("snap", "vert"),
            P(),
            P(),
            P(),
            P(),
            P(),
        ),
        out_specs=P("snap", "vert", None),
        check_vma=False,
    )
```

```python
import functools

import jax
import jax.numpy as jnp
from jax import lax
from jax.experimental import pallas as pl
from jax.experimental.pallas import tpu as pltpu
from jax.sharding import PartitionSpec as P

TILE = 128
TAPS = 16
RING = 8
SMEM = pl.BlockSpec(memory_space=pltpu.SMEM)
VMEM = pl.BlockSpec(memory_space=pltpu.VMEM)


def call(kernel, outs, operands, specs, flops, moved, aliases={}, scratch=()):
    return pl.pallas_call(
        kernel,
        out_shape=outs,
        in_specs=specs,
        out_specs=jax.tree.map(lambda _: VMEM, outs),
        scratch_shapes=scratch,
        input_output_aliases=aliases,
        cost_estimate=pl.CostEstimate(flops=flops, bytes_accessed=moved, transcendentals=0),
        compiler_params=pltpu.CompilerParams(vmem_limit_bytes=16 << 20),
    )(*operands)


def plan_kernel(slots, where, own, partner, plan):
    y, core = where[0] // 2, where[0] % 2
    lists = 2 * RING
    for i in range(lists):
        plan[i] = 0
    for side, table in enumerate((own, partner)):
        for r in range(2):

            @pl.loop(0, table[r * (slots + 1) + slots])
            def _(k):
                column = table[r * (slots + 1) + k]
                step = (column // 4 - y) * (1 - 2 * core)
                near = lax.rem(step + RING, RING) * 2 + side

                @pl.when(lax.rem(column // 2, 2) == core)
                def _():
                    filled = plan[near]
                    plan[lists + near * 2 * slots + filled] = (r * slots + k) * 2 + lax.rem(
                        column, 2
                    )
                    plan[near] = filled + 1


def add_tiles(plan, pieces, tiles, sums):
    for near, piece in pieces:
        for side in tiles:
            slots = tiles[side].shape[0] // 2
            index = near * 2 + side

            @pl.loop(0, plan[index])
            def _(i):
                entry = plan[2 * RING + index * 2 * slots + i]
                half, slot = lax.rem(entry, 2), entry // 2
                rows = pl.ds(pl.multiple_of(slot // slots * TILE, TILE), TILE)
                block = pl.ds(pl.multiple_of(half * TILE, TILE), TILE)
                sums[side][rows, :] += jnp.dot(
                    tiles[side][slot], piece[block, :], preferred_element_type=jnp.float32
                )


def early_kernel(plan, p0, p1, p2, p6, p7, own_tiles, other_tiles, w_root, mine, theirs, root):
    mine[...] = jnp.zeros_like(mine)
    theirs[...] = jnp.zeros_like(theirs)
    pieces = ((0, p0), (1, p1), (7, p7), (2, p2), (6, p6))
    add_tiles(plan, pieces, {0: own_tiles, 1: other_tiles}, {0: mine, 1: theirs})
    root[...] = jnp.dot(p0[...], w_root[...], preferred_element_type=jnp.float32)


def late_kernel(plan, p3, p4, p5, tiles, sums_in, sums, *, side):
    sums[...] = sums_in[...]
    add_tiles(plan, ((3, p3), (4, p4), (5, p5)), {side: tiles}, {side: sums})


def last_kernel(mine, received, root, w_message, out):
    total = (mine[...] + received[...]).astype(jnp.bfloat16)
    full = jnp.dot(total, w_message[...], preferred_element_type=jnp.float32) + root[...]
    out[...] = jnp.maximum(full, 0.0).astype(jnp.bfloat16)


def shift(x, distance):
    chips = range(RING)
    pairs = [(2 * y, (2 * y + 2 * distance) % (2 * RING)) for y in chips]
    pairs += [(2 * y + 1, (2 * y - 2 * distance) % (2 * RING) + 1) for y in chips]
    return lax.ppermute(x, "vert", pairs)


def swap(x):
    return lax.ppermute(x, "vert", [(v, v ^ 1) for v in range(2 * RING)])


def ring_gather(own):
    ahead2, back2 = shift(own, 2), shift(own, -2)
    ahead1, back1 = shift(own, 1), shift(own, -1)
    across = shift(ahead2, 2)
    ahead3, back3 = shift(ahead2, 1), shift(back2, -1)
    return (own, back1, back2, back3, across, ahead3, ahead2, ahead1)


def graph_layer(pieces, own_tiles, other_tiles, plan, w_message, w_root):
    own = pieces[0]
    rows, width = own.shape
    sums = jax.ShapeDtypeStruct((rows, width), jnp.float32)
    area = rows * width
    dense = 2 * area * width
    mine, theirs, root = call(
        early_kernel,
        (sums, sums, sums),
        (plan, own, pieces[1], pieces[2], pieces[6], pieces[7], own_tiles, other_tiles, w_root),
        [SMEM] + [VMEM] * 8,
        4 * dense,
        24 * area,
    )
    late = pieces[3:6]

    def finish(side, tiles, partial):
        return call(
            functools.partial(late_kernel, side=side),
            sums,
            (plan, *late, tiles, partial),
            [SMEM] + [VMEM] * 5,
            dense,
            8 * area,
            aliases={5: 0},
        )

    received = swap(finish(1, other_tiles, theirs))
    mine = finish(0, own_tiles, mine)
    return call(
        last_kernel,
        jax.ShapeDtypeStruct((rows, width), jnp.bfloat16),
        (mine, received, root, w_message),
        [VMEM] * 4,
        dense,
        14 * area,
    )


def filter_kernel(hidden, taps, out):
    steps = hidden.shape[0]
    for t in range(steps):
        acc = taps[0:1, :] * hidden[t].astype(jnp.float32)
        for j in range(1, min(TAPS - 1, t) + 1):
            acc = acc + taps[j : j + 1, :] * hidden[t - j].astype(jnp.float32)
        out[t] = acc.astype(jnp.bfloat16)


def temporal(hidden, taps):
    rows, width = hidden.shape
    steps = lax.axis_size("snap")
    split = hidden.reshape(steps, rows // steps, width)
    by_vertex = lax.all_to_all(split, "snap", split_axis=0, concat_axis=0)
    mixed = call(
        filter_kernel,
        jax.ShapeDtypeStruct(by_vertex.shape, jnp.bfloat16),
        (by_vertex, taps),
        [VMEM] * 2,
        32 * rows * width,
        4 * rows * width,
    )
    returned = lax.all_to_all(mixed, "snap", split_axis=0, concat_axis=0)
    return returned.reshape(rows, width)


def shards(
    features,
    tile_values,
    tile_column,
    tile_count,
    message_one,
    root_one,
    time_taps,
    message_two,
    root_two,
):
    slots = tile_column.shape[2]
    own_tiles = tile_values[0].reshape(2 * slots, TILE, TILE)
    table = jnp.concatenate([tile_column[0], tile_count[0][:, None]], 1).reshape(-1)
    pieces = ring_gather(features[0])
    other_tiles, other_table = swap(own_tiles), swap(table)
    plan = pl.pallas_call(
        functools.partial(plan_kernel, slots),
        out_shape=jax.ShapeDtypeStruct((2 * RING * (2 * slots + 1),), jnp.int32),
        in_specs=[SMEM] * 3,
        out_specs=SMEM,
        cost_estimate=pl.CostEstimate(flops=1000, bytes_accessed=4000, transcendentals=0),
        name="plan",
    )(lax.axis_index("vert").reshape(1), table, other_table)
    hidden = graph_layer(pieces, own_tiles, other_tiles, plan, message_one, root_one)
    mixed = temporal(hidden, time_taps)
    pieces = ring_gather(mixed)
    out = graph_layer(pieces, own_tiles, other_tiles, plan, message_two, root_two)
    return out[None]


def solution(mesh):
    return jax.shard_map(
        shards,
        mesh=mesh,
        in_specs=(
            P("snap", "vert", None),
            P("snap", "vert", None, None, None),
            P("snap", "vert", None),
            P("snap", "vert"),
            P(),
            P(),
            P(),
            P(),
            P(),
        ),
        out_specs=P("snap", "vert", None),
        check_vma=False,
    )
```

```python
import functools

import jax
import jax.numpy as jnp
from jax import lax
from jax.experimental import pallas as pl
from jax.experimental.pallas import tpu as pltpu
from jax.sharding import PartitionSpec as P

TILE = 128
TAPS = 16
RING = 8
SMEM = pl.BlockSpec(memory_space=pltpu.SMEM)
VMEM = pl.BlockSpec(memory_space=pltpu.VMEM)
HBM = pl.BlockSpec(memory_space=pltpu.HBM)


def call(kernel, outs, operands, specs, flops, moved, aliases={}, scratch=()):
    return pl.pallas_call(
        kernel,
        out_shape=outs,
        in_specs=specs,
        out_specs=jax.tree.map(lambda _: VMEM, outs),
        scratch_shapes=scratch,
        input_output_aliases=aliases,
        cost_estimate=pl.CostEstimate(flops=flops, bytes_accessed=moved, transcendentals=0),
        compiler_params=pltpu.CompilerParams(vmem_limit_bytes=16 << 20),
    )(*operands)


def plan_kernel(slots, where, own, partner, plan):
    y, core = where[0] // 2, where[0] % 2
    lists = 2 * RING
    for i in range(lists):
        plan[i] = 0
    for side, table in enumerate((own, partner)):
        for r in range(2):

            @pl.loop(0, table[r * (slots + 1) + slots])
            def _(k):
                column = table[r * (slots + 1) + k]
                step = (column // 4 - y) * (1 - 2 * core)
                near = lax.rem(step + RING, RING) * 2 + side

                @pl.when(lax.rem(column // 2, 2) == core)
                def _():
                    filled = plan[near]
                    plan[lists + near * 2 * slots + filled] = (r * slots + k) * 2 + lax.rem(
                        column, 2
                    )
                    plan[near] = filled + 1


def add_tiles(plan, pieces, tiles, sums):
    for near, piece in pieces:
        for side in tiles:
            slots = tiles[side].shape[0] // 2
            index = near * 2 + side

            @pl.loop(0, plan[index])
            def _(i):
                entry = plan[2 * RING + index * 2 * slots + i]
                half, slot = lax.rem(entry, 2), entry // 2
                rows = pl.ds(pl.multiple_of(slot // slots * TILE, TILE), TILE)
                block = pl.ds(pl.multiple_of(half * TILE, TILE), TILE)
                sums[side][rows, :] += jnp.dot(
                    tiles[side][slot], piece[block, :], preferred_element_type=jnp.float32
                )


def early_kernel(plan, p0, p1, p2, p6, p7, own_tiles, other_tiles, w_root, *refs, fetch):
    if fetch:
        mine, theirs, root, tiles, w_local, sems, rows = refs
        pairs = ((p0, rows), (own_tiles, tiles), (w_root, w_local))
    else:
        mine, theirs, root, w_local, sems = refs
        rows, tiles, pairs = p0, own_tiles, ((w_root, w_local),)
    copies = [
        pltpu.make_async_copy(source, target, sems.at[i])
        for i, (source, target) in enumerate(pairs)
    ]
    for copy in copies:
        copy.start()
    near = ((1, p1), (7, p7), (2, p2), (6, p6))
    theirs[...] = jnp.zeros_like(theirs)
    add_tiles(plan, near, {1: other_tiles}, {1: theirs})
    for copy in copies:
        copy.wait()
    root[...] = jnp.dot(rows[...], w_local[...], preferred_element_type=jnp.float32)
    mine[...] = jnp.zeros_like(mine)
    add_tiles(plan, near, {0: tiles}, {0: mine})
    add_tiles(plan, ((0, rows),), {0: tiles, 1: other_tiles}, {0: mine, 1: theirs})


def late_kernel(plan, p3, p4, p5, tiles, sums_in, sums, *, side):
    sums[...] = sums_in[...]
    add_tiles(plan, ((3, p3), (4, p4), (5, p5)), {side: tiles}, {side: sums})


def last_kernel(mine, received, root, w_message, out):
    total = (mine[...] + received[...]).astype(jnp.bfloat16)
    full = jnp.dot(total, w_message[...], preferred_element_type=jnp.float32) + root[...]
    out[...] = jnp.maximum(full, 0.0).astype(jnp.bfloat16)


def shift(x, distance):
    chips = range(RING)
    pairs = [(2 * y, (2 * y + 2 * distance) % (2 * RING)) for y in chips]
    pairs += [(2 * y + 1, (2 * y - 2 * distance) % (2 * RING) + 1) for y in chips]
    return lax.ppermute(x, "vert", pairs)


def swap(x):
    return lax.ppermute(x, "vert", [(v, v ^ 1) for v in range(2 * RING)])


def ring_gather(own):
    ahead2, back2 = shift(own, 2), shift(own, -2)
    ahead1, back1 = shift(own, 1), shift(own, -1)
    across = shift(ahead2, 2)
    ahead3, back3 = shift(ahead2, 1), shift(back2, -1)
    return (own, back1, back2, back3, across, ahead3, ahead2, ahead1)


def graph_layer(pieces, own_tiles, other_tiles, plan, w_message, w_root, fetch):
    own = pieces[0]
    rows, width = own.shape
    sums = jax.ShapeDtypeStruct((rows, width), jnp.float32)
    area = rows * width
    dense = 2 * area * width
    outs = [sums, sums, sums]
    scratch = [pltpu.VMEM(w_root.shape, w_root.dtype), pltpu.SemaphoreType.DMA((3,))]
    if fetch:
        outs.append(jax.ShapeDtypeStruct(own_tiles.shape, own_tiles.dtype))
        scratch.append(pltpu.VMEM(own.shape, own.dtype))
    local = HBM if fetch else VMEM
    w_root = pltpu.with_memory_space_constraint(w_root, pltpu.HBM)
    plan = pltpu.with_memory_space_constraint(plan, pltpu.HBM)
    if fetch:
        own, own_tiles = (pltpu.with_memory_space_constraint(x, pltpu.HBM) for x in (own, own_tiles))
    results = call(
        functools.partial(early_kernel, fetch=fetch),
        outs,
        (plan, own, pieces[1], pieces[2], pieces[6], pieces[7], own_tiles, other_tiles, w_root),
        [SMEM, local, VMEM, VMEM, VMEM, VMEM, local, VMEM, HBM],
        4 * dense,
        24 * area,
        scratch=scratch,
    )
    mine, theirs, root = results[:3]
    if fetch:
        own_tiles = results[3]
    late = pieces[3:6]

    def finish(side, tiles, partial):
        return call(
            functools.partial(late_kernel, side=side),
            sums,
            (plan, *late, tiles, partial),
            [SMEM] + [VMEM] * 5,
            dense,
            8 * area,
            aliases={5: 0},
        )

    received = swap(finish(1, other_tiles, theirs))
    mine = finish(0, own_tiles, mine)
    out = call(
        last_kernel,
        jax.ShapeDtypeStruct((rows, width), jnp.bfloat16),
        (mine, received, root, w_message),
        [VMEM] * 4,
        dense,
        14 * area,
    )
    return out, own_tiles


def filter_kernel(hidden, taps, out):
    steps = hidden.shape[0]
    for t in range(steps):
        acc = taps[0:1, :] * hidden[t].astype(jnp.float32)
        for j in range(1, min(TAPS - 1, t) + 1):
            acc = acc + taps[j : j + 1, :] * hidden[t - j].astype(jnp.float32)
        out[t] = acc.astype(jnp.bfloat16)


def temporal(hidden, taps):
    rows, width = hidden.shape
    steps = lax.axis_size("snap")
    split = hidden.reshape(steps, rows // steps, width)
    by_vertex = lax.all_to_all(split, "snap", split_axis=0, concat_axis=0)
    mixed = call(
        filter_kernel,
        jax.ShapeDtypeStruct(by_vertex.shape, jnp.bfloat16),
        (by_vertex, taps),
        [VMEM] * 2,
        32 * rows * width,
        4 * rows * width,
    )
    returned = lax.all_to_all(mixed, "snap", split_axis=0, concat_axis=0)
    return returned.reshape(rows, width)


def shards(
    features,
    tile_values,
    tile_column,
    tile_count,
    message_one,
    root_one,
    time_taps,
    message_two,
    root_two,
):
    slots = tile_column.shape[2]
    own_tiles = tile_values[0].reshape(2 * slots, TILE, TILE)
    table = jnp.concatenate([tile_column[0], tile_count[0][:, None]], 1).reshape(-1)
    pieces = ring_gather(features[0])
    other_tiles, other_table = swap(own_tiles), swap(table)
    plan = pl.pallas_call(
        functools.partial(plan_kernel, slots),
        out_shape=jax.ShapeDtypeStruct((2 * RING * (2 * slots + 1),), jnp.int32),
        in_specs=[SMEM] * 3,
        out_specs=SMEM,
        cost_estimate=pl.CostEstimate(flops=1000, bytes_accessed=4000, transcendentals=0),
        name="plan",
    )(lax.axis_index("vert").reshape(1), table, other_table)
    hidden, own_tiles = graph_layer(
        pieces, own_tiles, other_tiles, plan, message_one, root_one, True
    )
    mixed = temporal(hidden, time_taps)
    pieces = ring_gather(mixed)
    out, _ = graph_layer(pieces, own_tiles, other_tiles, plan, message_two, root_two, False)
    return out[None]


def solution(mesh):
    return jax.shard_map(
        shards,
        mesh=mesh,
        in_specs=(
            P("snap", "vert", None),
            P("snap", "vert", None, None, None),
            P("snap", "vert", None),
            P("snap", "vert"),
            P(),
            P(),
            P(),
            P(),
            P(),
        ),
        out_specs=P("snap", "vert", None),
        check_vma=False,
    )
```

```python
import functools

import jax
import jax.numpy as jnp
from jax import lax
from jax.experimental import pallas as pl
from jax.experimental.pallas import tpu as pltpu
from jax.sharding import PartitionSpec as P

TILE = 128
TAPS = 16
RING = 8
SMEM = pl.BlockSpec(memory_space=pltpu.SMEM)
VMEM = pl.BlockSpec(memory_space=pltpu.VMEM)
HBM = pl.BlockSpec(memory_space=pltpu.HBM)


def call(kernel, outs, operands, specs, flops, moved, aliases={}, scratch=()):
    return pl.pallas_call(
        kernel,
        out_shape=outs,
        in_specs=specs,
        out_specs=jax.tree.map(lambda _: VMEM, outs),
        scratch_shapes=scratch,
        input_output_aliases=aliases,
        cost_estimate=pl.CostEstimate(flops=flops, bytes_accessed=moved, transcendentals=0),
        compiler_params=pltpu.CompilerParams(vmem_limit_bytes=16 << 20),
    )(*operands)


def plan_kernel(slots, where, own, partner, plan):
    y, core = where[0] >> 1, where[0] & 1
    lists = 2 * RING
    for i in range(lists):
        plan[i] = 0
    for side, table in enumerate((own, partner)):
        for r in range(2):

            @pl.loop(0, table[r * (slots + 1) + slots])
            def _(k):
                column = table[r * (slots + 1) + k]
                near = (((column >> 2) - y) * (1 - 2 * core)) & (RING - 1)
                index = near * 2 + side

                @pl.when(((column >> 1) & 1) == core)
                def _():
                    filled = plan[index]
                    plan[lists + index * 2 * slots + filled] = (
                        ((r * slots + k) << 2) + r * 2 + (column & 1)
                    )
                    plan[index] = filled + 1


def add_tiles(plan, pieces, tiles, sums):
    for near, piece in pieces:
        for side in tiles:
            slots = tiles[side].shape[0] // 2
            index = near * 2 + side

            @pl.loop(0, plan[index])
            def _(i):
                entry = plan[2 * RING + index * 2 * slots + i]
                rows = pl.ds(pl.multiple_of(((entry >> 1) & 1) * TILE, TILE), TILE)
                block = pl.ds(pl.multiple_of((entry & 1) * TILE, TILE), TILE)
                sums[side][rows, :] += jnp.dot(
                    tiles[side][entry >> 2], piece[block, :], preferred_element_type=jnp.float32
                )


def early_kernel(plan, p0, p1, p2, p6, p7, own_tiles, other_tiles, w_root, *refs, fetch):
    if fetch:
        mine, theirs, root, tiles, w_local, sems, rows = refs
        pairs = ((p0, rows), (own_tiles, tiles), (w_root, w_local))
    else:
        mine, theirs, root, w_local, sems = refs
        rows, tiles, pairs = p0, own_tiles, ((w_root, w_local),)
    copies = [
        pltpu.make_async_copy(source, target, sems.at[i])
        for i, (source, target) in enumerate(pairs)
    ]
    for copy in copies:
        copy.start()
    near = ((1, p1), (7, p7), (2, p2), (6, p6))
    theirs[...] = jnp.zeros_like(theirs)
    add_tiles(plan, near, {1: other_tiles}, {1: theirs})
    for copy in copies:
        copy.wait()
    root[...] = jnp.dot(rows[...], w_local[...], preferred_element_type=jnp.float32)
    mine[...] = jnp.zeros_like(mine)
    add_tiles(plan, near, {0: tiles}, {0: mine})
    add_tiles(plan, ((0, rows),), {0: tiles, 1: other_tiles}, {0: mine, 1: theirs})


def late_kernel(plan, p3, p4, p5, tiles, sums_in, sums, *, side):
    sums[...] = sums_in[...]
    add_tiles(plan, ((3, p3), (4, p4), (5, p5)), {side: tiles}, {side: sums})


def last_kernel(mine, received, root, w_message, out):
    total = (mine[...] + received[...]).astype(jnp.bfloat16)
    full = jnp.dot(total, w_message[...], preferred_element_type=jnp.float32) + root[...]
    out[...] = jnp.maximum(full, 0.0).astype(jnp.bfloat16)


def shift(x, distance):
    chips = range(RING)
    pairs = [(2 * y, (2 * y + 2 * distance) % (2 * RING)) for y in chips]
    pairs += [(2 * y + 1, (2 * y - 2 * distance) % (2 * RING) + 1) for y in chips]
    return lax.ppermute(x, "vert", pairs)


def swap(x):
    return lax.ppermute(x, "vert", [(v, v ^ 1) for v in range(2 * RING)])


def ring_gather(own):
    ahead2, back2 = shift(own, 2), shift(own, -2)
    ahead1, back1 = shift(own, 1), shift(own, -1)
    across = shift(ahead2, 2)
    ahead3, back3 = shift(ahead2, 1), shift(back2, -1)
    return (own, back1, back2, back3, across, ahead3, ahead2, ahead1)


def graph_layer(pieces, own_tiles, other_tiles, plan, w_message, w_root, fetch):
    own = pieces[0]
    rows, width = own.shape
    sums = jax.ShapeDtypeStruct((rows, width), jnp.float32)
    area = rows * width
    dense = 2 * area * width
    outs = [sums, sums, sums]
    scratch = [pltpu.VMEM(w_root.shape, w_root.dtype), pltpu.SemaphoreType.DMA((3,))]
    if fetch:
        outs.append(jax.ShapeDtypeStruct(own_tiles.shape, own_tiles.dtype))
        scratch.append(pltpu.VMEM(own.shape, own.dtype))
    local = HBM if fetch else VMEM
    w_root = pltpu.with_memory_space_constraint(w_root, pltpu.HBM)
    plan = pltpu.with_memory_space_constraint(plan, pltpu.HBM)
    if fetch:
        own, own_tiles = (pltpu.with_memory_space_constraint(x, pltpu.HBM) for x in (own, own_tiles))
    results = call(
        functools.partial(early_kernel, fetch=fetch),
        outs,
        (plan, own, pieces[1], pieces[2], pieces[6], pieces[7], own_tiles, other_tiles, w_root),
        [SMEM, local, VMEM, VMEM, VMEM, VMEM, local, VMEM, HBM],
        4 * dense,
        24 * area,
        scratch=scratch,
    )
    mine, theirs, root = results[:3]
    if fetch:
        own_tiles = results[3]
    late = pieces[3:6]

    def finish(side, tiles, partial):
        return call(
            functools.partial(late_kernel, side=side),
            sums,
            (plan, *late, tiles, partial),
            [SMEM] + [VMEM] * 5,
            dense,
            8 * area,
            aliases={5: 0},
        )

    received = swap(finish(1, other_tiles, theirs))
    mine = finish(0, own_tiles, mine)
    out = call(
        last_kernel,
        jax.ShapeDtypeStruct((rows, width), jnp.bfloat16),
        (mine, received, root, w_message),
        [VMEM] * 4,
        dense,
        14 * area,
    )
    return out, own_tiles


def filter_kernel(hidden, taps, out):
    steps = hidden.shape[0]
    for t in range(steps):
        acc = taps[0:1, :] * hidden[t].astype(jnp.float32)
        for j in range(1, min(TAPS - 1, t) + 1):
            acc = acc + taps[j : j + 1, :] * hidden[t - j].astype(jnp.float32)
        out[t] = acc.astype(jnp.bfloat16)


def temporal(hidden, taps):
    rows, width = hidden.shape
    steps = lax.axis_size("snap")
    split = hidden.reshape(steps, rows // steps, width)
    by_vertex = lax.all_to_all(split, "snap", split_axis=0, concat_axis=0)
    mixed = call(
        filter_kernel,
        jax.ShapeDtypeStruct(by_vertex.shape, jnp.bfloat16),
        (by_vertex, taps),
        [VMEM] * 2,
        32 * rows * width,
        4 * rows * width,
    )
    returned = lax.all_to_all(mixed, "snap", split_axis=0, concat_axis=0)
    return returned.reshape(rows, width)


def shards(
    features,
    tile_values,
    tile_column,
    tile_count,
    message_one,
    root_one,
    time_taps,
    message_two,
    root_two,
):
    slots = tile_column.shape[2]
    own_tiles = tile_values[0].reshape(2 * slots, TILE, TILE)
    table = jnp.concatenate([tile_column[0], tile_count[0][:, None]], 1).reshape(-1)
    pieces = ring_gather(features[0])
    other_tiles, other_table = swap(own_tiles), swap(table)
    plan = pl.pallas_call(
        functools.partial(plan_kernel, slots),
        out_shape=jax.ShapeDtypeStruct((2 * RING * (2 * slots + 1),), jnp.int32),
        in_specs=[SMEM] * 3,
        out_specs=SMEM,
        cost_estimate=pl.CostEstimate(flops=1000, bytes_accessed=4000, transcendentals=0),
        name="plan",
    )(lax.axis_index("vert").reshape(1), table, other_table)
    hidden, own_tiles = graph_layer(
        pieces, own_tiles, other_tiles, plan, message_one, root_one, True
    )
    mixed = temporal(hidden, time_taps)
    pieces = ring_gather(mixed)
    out, _ = graph_layer(pieces, own_tiles, other_tiles, plan, message_two, root_two, False)
    return out[None]


def solution(mesh):
    return jax.shard_map(
        shards,
        mesh=mesh,
        in_specs=(
            P("snap", "vert", None),
            P("snap", "vert", None, None, None),
            P("snap", "vert", None),
            P("snap", "vert"),
            P(),
            P(),
            P(),
            P(),
            P(),
        ),
        out_specs=P("snap", "vert", None),
        check_vma=False,
    )
```

```python
import functools

import jax
import jax.numpy as jnp
from jax import lax
from jax.experimental import pallas as pl
from jax.experimental.pallas import tpu as pltpu
from jax.sharding import PartitionSpec as P

TILE = 128
TAPS = 16
RING = 8
SMEM = pl.BlockSpec(memory_space=pltpu.SMEM)
VMEM = pl.BlockSpec(memory_space=pltpu.VMEM)
HBM = pl.BlockSpec(memory_space=pltpu.HBM)


def call(kernel, outs, operands, specs, flops, moved, aliases={}, scratch=()):
    return pl.pallas_call(
        kernel,
        out_shape=outs,
        in_specs=specs,
        out_specs=jax.tree.map(lambda _: VMEM, outs),
        scratch_shapes=scratch,
        input_output_aliases=aliases,
        cost_estimate=pl.CostEstimate(flops=flops, bytes_accessed=moved, transcendentals=0),
        compiler_params=pltpu.CompilerParams(vmem_limit_bytes=16 << 20),
    )(*operands)


def plan_kernel(slots, where, own, partner, plan):
    y, core = where[0] >> 1, where[0] & 1
    lists = 2 * RING
    for i in range(lists):
        plan[i] = 0
    for side, table in enumerate((own, partner)):
        for r in range(2):

            @pl.loop(0, table[r * (slots + 1) + slots])
            def _(k):
                column = table[r * (slots + 1) + k]
                near = (((column >> 2) - y) * (1 - 2 * core)) & (RING - 1)
                index = near * 2 + side

                @pl.when(((column >> 1) & 1) == core)
                def _():
                    filled = plan[index]
                    plan[lists + index * 2 * slots + filled] = (
                        ((r * slots + k) << 2) + r * 2 + (column & 1)
                    )
                    plan[index] = filled + 1


def add_tiles(plan, pieces, tiles, sums):
    for near, piece in pieces:
        for side in tiles:
            slots = tiles[side].shape[0] // 2
            index = near * 2 + side

            @pl.loop(0, plan[index])
            def _(i):
                entry = plan[2 * RING + index * 2 * slots + i]
                rows = pl.ds(pl.multiple_of(((entry >> 1) & 1) * TILE, TILE), TILE)
                block = pl.ds(pl.multiple_of((entry & 1) * TILE, TILE), TILE)
                sums[side][rows, :] += jnp.dot(
                    tiles[side][entry >> 2], piece[block, :], preferred_element_type=jnp.float32
                )


def early_kernel(plan, p0, p1, p2, p6, p7, own_tiles, other_tiles, w_root, *refs, fetch):
    if fetch:
        mine, theirs, root, tiles, w_local, sems, rows = refs
        pairs = ((p0, rows), (own_tiles, tiles), (w_root, w_local))
    else:
        mine, theirs, root, w_local, sems = refs
        rows, tiles, pairs = p0, own_tiles, ((w_root, w_local),)
    copies = [
        pltpu.make_async_copy(source, target, sems.at[i])
        for i, (source, target) in enumerate(pairs)
    ]
    for copy in copies:
        copy.start()
    near = ((1, p1), (7, p7), (2, p2), (6, p6))
    theirs[...] = jnp.zeros_like(theirs)
    add_tiles(plan, near, {1: other_tiles}, {1: theirs})
    for copy in copies:
        copy.wait()
    root[...] = jnp.dot(rows[...], w_local[...], preferred_element_type=jnp.float32)
    mine[...] = jnp.zeros_like(mine)
    add_tiles(plan, near, {0: tiles}, {0: mine})
    add_tiles(plan, ((0, rows),), {0: tiles, 1: other_tiles}, {0: mine, 1: theirs})


def late_kernel(plan, p3, p4, p5, tiles, sums_in, sums, *, side):
    sums[...] = sums_in[...]
    add_tiles(plan, ((3, p3), (4, p4), (5, p5)), {side: tiles}, {side: sums})


def last_kernel(mine, received, root, w_message, out):
    size = out.shape[0]
    rows = pl.ds(pl.multiple_of(pl.program_id(0) * size, size), size)
    total = (mine[rows, :] + received[rows, :]).astype(jnp.bfloat16)
    full = jnp.dot(total, w_message[...], preferred_element_type=jnp.float32) + root[rows, :]
    out[...] = jnp.maximum(full, 0.0).astype(jnp.bfloat16)


def shift(x, distance):
    chips = range(RING)
    pairs = [(2 * y, (2 * y + 2 * distance) % (2 * RING)) for y in chips]
    pairs += [(2 * y + 1, (2 * y - 2 * distance) % (2 * RING) + 1) for y in chips]
    return lax.ppermute(x, "vert", pairs)


def swap(x):
    return lax.ppermute(x, "vert", [(v, v ^ 1) for v in range(2 * RING)])


def ring_gather(own):
    ahead2, back2 = shift(own, 2), shift(own, -2)
    ahead1, back1 = shift(own, 1), shift(own, -1)
    across = shift(ahead2, 2)
    ahead3, back3 = shift(ahead2, 1), shift(back2, -1)
    return (own, back1, back2, back3, across, ahead3, ahead2, ahead1)


def graph_layer(pieces, own_tiles, other_tiles, plan, w_message, w_root, fetch):
    own = pieces[0]
    rows, width = own.shape
    sums = jax.ShapeDtypeStruct((rows, width), jnp.float32)
    area = rows * width
    dense = 2 * area * width
    outs = [sums, sums, sums]
    scratch = [pltpu.VMEM(w_root.shape, w_root.dtype), pltpu.SemaphoreType.DMA((3,))]
    if fetch:
        outs.append(jax.ShapeDtypeStruct(own_tiles.shape, own_tiles.dtype))
        scratch.append(pltpu.VMEM(own.shape, own.dtype))
    local = HBM if fetch else VMEM
    w_root = pltpu.with_memory_space_constraint(w_root, pltpu.HBM)
    plan = pltpu.with_memory_space_constraint(plan, pltpu.HBM)
    if fetch:
        own, own_tiles = (pltpu.with_memory_space_constraint(x, pltpu.HBM) for x in (own, own_tiles))
    results = call(
        functools.partial(early_kernel, fetch=fetch),
        outs,
        (plan, own, pieces[1], pieces[2], pieces[6], pieces[7], own_tiles, other_tiles, w_root),
        [SMEM, local, VMEM, VMEM, VMEM, VMEM, local, VMEM, HBM],
        4 * dense,
        24 * area,
        scratch=scratch,
    )
    mine, theirs, root = results[:3]
    if fetch:
        own_tiles = results[3]
    late = pieces[3:6]

    def finish(side, tiles, partial):
        return call(
            functools.partial(late_kernel, side=side),
            sums,
            (plan, *late, tiles, partial),
            [SMEM] + [VMEM] * 5,
            dense,
            8 * area,
            aliases={5: 0},
        )

    received = swap(finish(1, other_tiles, theirs))
    mine = finish(0, own_tiles, mine)
    blocks = 1 if fetch else 2
    out = pl.pallas_call(
        last_kernel,
        out_shape=jax.ShapeDtypeStruct((rows, width), jnp.bfloat16),
        grid=(blocks,),
        in_specs=[VMEM] * 4,
        out_specs=pl.BlockSpec((rows // blocks, width), lambda i: (i, 0)),
        cost_estimate=pl.CostEstimate(flops=dense, bytes_accessed=14 * area, transcendentals=0),
        compiler_params=pltpu.CompilerParams(vmem_limit_bytes=16 << 20),
        name="last",
    )(mine, received, root, w_message)
    return out, own_tiles


def filter_kernel(hidden, taps, out):
    steps = hidden.shape[0]
    for t in range(steps):
        acc = taps[0:1, :] * hidden[t].astype(jnp.float32)
        for j in range(1, min(TAPS - 1, t) + 1):
            acc = acc + taps[j : j + 1, :] * hidden[t - j].astype(jnp.float32)
        out[t] = acc.astype(jnp.bfloat16)


def temporal(hidden, taps):
    rows, width = hidden.shape
    steps = lax.axis_size("snap")
    split = hidden.reshape(steps, rows // steps, width)
    by_vertex = lax.all_to_all(split, "snap", split_axis=0, concat_axis=0)
    mixed = call(
        filter_kernel,
        jax.ShapeDtypeStruct(by_vertex.shape, jnp.bfloat16),
        (by_vertex, taps),
        [VMEM] * 2,
        32 * rows * width,
        4 * rows * width,
    )
    returned = lax.all_to_all(mixed, "snap", split_axis=0, concat_axis=0)
    return returned.reshape(rows, width)


def shards(
    features,
    tile_values,
    tile_column,
    tile_count,
    message_one,
    root_one,
    time_taps,
    message_two,
    root_two,
):
    slots = tile_column.shape[2]
    own_tiles = tile_values[0].reshape(2 * slots, TILE, TILE)
    table = jnp.concatenate([tile_column[0], tile_count[0][:, None]], 1).reshape(-1)
    pieces = ring_gather(features[0])
    other_tiles, other_table = swap(own_tiles), swap(table)
    plan = pl.pallas_call(
        functools.partial(plan_kernel, slots),
        out_shape=jax.ShapeDtypeStruct((2 * RING * (2 * slots + 1),), jnp.int32),
        in_specs=[SMEM] * 3,
        out_specs=SMEM,
        cost_estimate=pl.CostEstimate(flops=1000, bytes_accessed=4000, transcendentals=0),
        name="plan",
    )(lax.axis_index("vert").reshape(1), table, other_table)
    hidden, own_tiles = graph_layer(
        pieces, own_tiles, other_tiles, plan, message_one, root_one, True
    )
    mixed = temporal(hidden, time_taps)
    pieces = ring_gather(mixed)
    out, _ = graph_layer(pieces, own_tiles, other_tiles, plan, message_two, root_two, False)
    return out[None]


def solution(mesh):
    return jax.shard_map(
        shards,
        mesh=mesh,
        in_specs=(
            P("snap", "vert", None),
            P("snap", "vert", None, None, None),
            P("snap", "vert", None),
            P("snap", "vert"),
            P(),
            P(),
            P(),
            P(),
            P(),
        ),
        out_specs=P("snap", "vert", None),
        check_vma=False,
    )
```
